32 devices in a mesh: blk: 4 (over z), slab: 8 (over y, x, core).
Axes of the slice: x: 2, y: 2, z: 4, core: 2. Of those that a mesh axis runs over, the one named last changes fastest.
Arguments:
- new_rows: bfloat16 [16384, 768], P(('blk', 'slab')), may hold values from -6 to 6
- index_rows: bfloat16 [16384, 768], P('blk'), may hold values from -6 to 6
- pattern: int32 [32, 4], replicated, may hold values from 0 to 1, as said below
- kept_row: int32 [8192], P(('blk', 'slab')), may hold values from 0 to 511
- kept_owner: int32 [8192, 1], P(('blk', 'slab')), may hold values from 0 to 31; in each aligned block of 256 rows (0 to 255, 256 to 511, ...) at most 16 rows name the same one
- kept_local: int32 [8192], P(('blk', 'slab')), may hold values from 0 to 15
Outputs:
- best_cosine: float32 [16384], P(('blk', 'slab'))
- centroid_sums: float32 [512, 768], P(('blk', 'slab'))
- kept_counts: float32 [512], P(('blk', 'slab'))
The draws below stay inside these ranges and needn't reach their ends.
Inputs may be any that keep to these rules, and one draw needn't show every extreme that they name: `pattern`: every row has at least one 1. `kept_owner`: the 256 entries of one device name one owner at most 16 times, a bound that some block reaches.
All inputs are finite; a program needn't handle non-finite values.
Results may differ from the reference program's by a relative error of at most 0.0029.
Values may be sent and summed in bfloat16 or wider, within the bound.
No kernel may reach another device: no remote copies, remote signals or barrier semaphores. Data moves between devices by JAX's collectives and lax.ppermute only.
A program may use at most 64 MiB of HBM per device.

```python
import math
import jax
import jax.numpy as jnp
import numpy as np
from jax import lax

D = 768
NEW_DEV = 512
IDX_BLK = 4096
KEEP_DEV = 256
CL_DEV = 16
KCAP = 16
NEW_BLOCKS = 32
IDX_BLOCKS = 4
NEW = 16384
IDX = 16384
NCLUS = 512
KEEP = 8192
DEVICES = 32


def draw_pattern(key, part):
    key_level, key_noise, key_pick = jax.random.split(jax.random.fold_in(key, 17), 3)
    level = jax.random.randint(key_level, (NEW_BLOCKS, 1), 1, IDX_BLOCKS + 1)
    noise = jax.random.randint(key_noise, (NEW_BLOCKS, IDX_BLOCKS), 0, IDX_BLOCKS)
    chosen = jax.random.randint(key_pick, (NEW_BLOCKS, 1), 0, IDX_BLOCKS)
    columns = jnp.arange(IDX_BLOCKS, dtype=jnp.int32)[None, :]
    return ((noise < level) | (columns == chosen)).astype(jnp.int32)


def place_ends(values, stream_key, low, largest):
    longest = values.shape.index(max(values.shape))
    spots = []
    for shift in (0, 1):
        where = [jax.random.randint(jax.random.fold_in(stream_key, axis), (), 0, length) for axis, length in enumerate(values.shape)]
        where[longest] = (where[longest] + shift) % values.shape[longest]
        spots.append(tuple(where))
    return values.at[spots[0]].set(low).at[spots[1]].set(largest)


def block_levels(key, dims, shards, low, top_value):
    def one(position, parts):
        draws = jax.random.uniform(jax.random.fold_in(jax.random.fold_in(key, 6), position), (parts,), jnp.float32, low / len(shards), top_value / len(shards))
        return jnp.repeat(jnp.exp(draws), dims[position] // parts).reshape((-1,) + (1,) * (len(dims) - position - 1))

    factor_of = one(*shards[0])
    for cut in shards[1:]:
        factor_of = factor_of * one(*cut)
    return factor_of


def deal_out(rng, own, number, rows, amount, top, bound, skew):
    ranking = jax.random.permutation(rng, amount)
    crowded, ordinary = load_shares(amount, rows * top, bound, skew, True), load_shares(amount, rows * top, bound, skew, False)
    places = jnp.arange(amount)

    def named(sizes, rotation):
        used = int((sizes > 0).sum())
        fixed = max(1, used // 4)
        shifted = fixed + (places - fixed + rotation * (used - fixed)) % max(1, amount - fixed)
        return jnp.zeros((amount,), jnp.int32).at[ranking[jnp.where(places < fixed, places, shifted)]].set(jnp.asarray(sizes, jnp.int32))

    sizes = jnp.where(number % 4 == 0, named(crowded, number // 4), named(ordinary, number - number // 4 - 1))
    mixed = jax.random.permutation(jax.random.fold_in(own, 3), amount)
    giver, taker = mixed[0:amount // 2 * 2:2], mixed[1:amount // 2 * 2:2]
    margin = jnp.minimum(sizes[giver] - 1, bound - sizes[taker]) // 2
    margin = jnp.where((giver == ranking[0]) | (taker == ranking[0]) | (sizes[taker] == 0), 0, jnp.maximum(margin, 0))
    shifted = jax.random.randint(jax.random.fold_in(own, 4), (amount // 2,), 0, 1 << 20) % (margin + 1)
    sizes = sizes.at[giver].add(-shifted).at[taker].add(shifted)
    members = jnp.searchsorted(jnp.cumsum(sizes), jnp.arange(rows * top), side="right").astype(jnp.int32)
    table = members.reshape(top, rows).T
    table = table[jax.random.permutation(jax.random.fold_in(own, 1), rows)]
    rotation = jax.random.randint(jax.random.fold_in(own, 2), (rows, 1), 0, top)
    return jnp.take_along_axis(table, (jnp.arange(top)[None, :] + rotation) % top, axis=1)


def load_shares(amount, total, bound, lean, full):
    weights = [(1 << 20) // math.isqrt(standing ** lean) + 1 for standing in range(1, amount + 1)]
    largest = bound if full else min(bound, max(-(-total // amount), total * weights[0] // sum(weights)))
    least = 1 if total - largest >= amount - 1 else 0
    holding, spare = [largest] + [least] * (amount - 1), total - largest - least * (amount - 1)
    while spare > 0:
        free = [i for i in range(1, amount) if holding[i] < largest] or [i for i in range(1, amount) if holding[i] < bound]
        whole, left = sum([weights[i] for i in free]), spare
        for i in free:
            more = min(bound - holding[i], max(1, left * weights[i] // whole), spare)
            holding[i] = holding[i] + more
            spare = spare - more
    return np.array(holding)


def bell_draw(key, dims, spread, reach, pieces=(), kind=jnp.bfloat16):
    values = jax.random.normal(key, dims, jnp.float32) * spread
    if len(pieces) > 0:
        values = block_levels(key, dims, pieces, -0.22, 0.18) * values
    return jnp.clip(values, min=-reach, max=reach).astype(kind)


def setup_inputs(seed: int = 0) -> dict:
    arg_keys = jax.random.split(jax.random.key(seed), 7)
    new_rows = bell_draw(arg_keys[0], (NEW, D), 1.0, 6.0, ((0, 32),))
    index_rows = bell_draw(arg_keys[1], (IDX, D), 1.0, 6.0, ((0, 4),))
    pattern = draw_pattern(jax.random.fold_in(arg_keys[6], 71), 0)
    kept_row = place_ends(jax.random.randint(arg_keys[3], (KEEP,), 0, NEW_DEV), jax.random.fold_in(arg_keys[3], 1), 0, NEW_DEV - 1).astype(jnp.int32)
    kept_owner_keys = jax.random.split(jax.random.fold_in(arg_keys[4], 1), KEEP // KEEP_DEV)
    kept_owner_turns = jax.random.permutation(jax.random.fold_in(arg_keys[4], 3), KEEP // KEEP_DEV)
    kept_owner = jax.vmap(lambda own, number: deal_out(jax.random.fold_in(arg_keys[4], 2), own, number, KEEP_DEV, DEVICES, 1, KCAP, 2))(kept_owner_keys, kept_owner_turns).reshape((KEEP, 1))
    kept_local = place_ends(jax.random.randint(arg_keys[5], (KEEP,), 0, CL_DEV), jax.random.fold_in(arg_keys[5], 1), 0, CL_DEV - 1).astype(jnp.int32)
    return {"new_rows": new_rows, "index_rows": index_rows, "pattern": pattern, "kept_row": kept_row, "kept_owner": kept_owner, "kept_local": kept_local}


EPS = 1e-06

def unit_rows(values):
    wide = values.astype(jnp.float32)
    scale = lax.rsqrt(lax.optimization_barrier(jnp.sum(wide * wide, axis=-1, keepdims=True)) + EPS)
    return (wide * scale).astype(jnp.bfloat16)

def reference(new_rows, index_rows, pattern, kept_row, kept_owner, kept_local):
    new_unit = unit_rows(new_rows)
    index_unit = unit_rows(index_rows)
    blocks = new_unit.reshape(NEW_BLOCKS, NEW_DEV, D)
    col_block = jnp.arange(IDX, dtype=jnp.int32) // IDX_BLK

    def block_max(args):
        rows, marks = args
        scores = lax.dot_general(rows, index_unit, (((1,), (1,)), ((), ())), preferred_element_type=jnp.float32)
        live = marks[col_block] > 0
        masked = jnp.where(live[None, :], scores, jnp.float32(-2.0))
        return lax.optimization_barrier(jnp.max(masked, axis=1))
    best = lax.map(block_max, (blocks, pattern)).reshape(NEW)
    entry = jnp.arange(KEEP, dtype=jnp.int32)
    global_row = entry // KEEP_DEV * NEW_DEV + kept_row.astype(jnp.int32)
    picked = new_unit[global_row].astype(jnp.float32)
    cluster = (kept_owner[:, 0] * CL_DEV + kept_local).astype(jnp.int32)
    sums = jax.ops.segment_sum(picked, cluster, num_segments=NCLUS)
    counts = jax.ops.segment_sum(jnp.ones((KEEP,), jnp.float32), cluster, num_segments=NCLUS)
    return (best, sums, counts)
```

```python
import jax
import jax.numpy as jnp
from jax import lax
from jax.sharding import PartitionSpec as P


CL_DEV = 16
EPS = 1e-06
PIECES = 2
LANES = 128


def shifted(value, axis, steps):
    count = lax.axis_size(axis)
    pairs = [(source, (source + steps) % count) for source in range(count)]
    return lax.ppermute(value, axis, pairs)


def inverse_norm(values):
    wide = values.astype(jnp.float32)
    return lax.rsqrt(jnp.sum(wide * wide, axis=-1, keepdims=True) + EPS)


def unit_rows(values):
    return (values.astype(jnp.float32) * inverse_norm(values)).astype(jnp.bfloat16)


def kept_sums(new_unit, kept_row, owner, kept_local):
    cycle = lax.axis_size("blk")
    lanes = lax.axis_size("slab")
    rows, width = new_unit.shape
    entries = kept_row.shape[0]
    pick = (kept_row[:, None] == jnp.arange(rows, dtype=jnp.int32)[None, :]).astype(jnp.bfloat16)
    picked = jnp.dot(pick, new_unit, preferred_element_type=jnp.float32).astype(jnp.bfloat16)
    picked = jnp.concatenate([picked, jnp.ones((entries, LANES), jnp.bfloat16)], axis=1)
    place = ((owner % lanes) * cycle + owner // lanes) * CL_DEV + kept_local
    spread = (jnp.arange(lanes * cycle * CL_DEV, dtype=jnp.int32)[:, None] == place[None, :]).astype(
        jnp.bfloat16
    )
    part = jnp.dot(spread, picked, preferred_element_type=jnp.float32)
    part = part.reshape(lanes, cycle * CL_DEV, width + LANES)
    part = lax.all_to_all(part, "slab", split_axis=0, concat_axis=0, tiled=True)
    part = jnp.sum(part, axis=0).astype(jnp.bfloat16)
    part = part.reshape(cycle, CL_DEV, width + LANES)
    part = lax.all_to_all(part, "blk", split_axis=0, concat_axis=0, tiled=True)
    total = jnp.sum(part.astype(jnp.float32), axis=0)
    return total[:, :width], total[:, width]


def per_device(new_rows, index_rows, pattern, kept_row, kept_owner, kept_local):
    cycle = lax.axis_size("blk")
    lanes = lax.axis_size("slab")
    here = lax.axis_index("blk")
    lane = lax.axis_index("slab")
    index_unit = unit_rows(index_rows)

    def tile_max(rows):
        scores = lax.dot_general(
            rows, index_unit, (((1,), (1,)), ((), ())), preferred_element_type=jnp.float32
        )
        return jnp.max(scores, axis=1)

    piece = new_rows.shape[0] // PIECES
    moving = [new_rows[i * piece : (i + 1) * piece] for i in range(PIECES)]
    home = [tile_max(new_rows)]
    for step in range(1, cycle):
        tops = []
        for i in range(PIECES):
            moving[i] = shifted(moving[i], "blk", 1)
            tops.append(tile_max(moving[i]))
        home.append(shifted(jnp.concatenate(tops), "blk", -step))
    scale = lax.optimization_barrier(inverse_norm(new_rows))
    sums, counts = kept_sums(
        (new_rows.astype(jnp.float32) * scale).astype(jnp.bfloat16),
        kept_row,
        kept_owner[:, 0],
        kept_local,
    )
    marks = lax.dynamic_slice_in_dim(pattern, here * lanes + lane, 1, axis=0)[0]
    best = jnp.full((new_rows.shape[0],), -2.0, jnp.float32)
    for step in range(cycle):
        live = marks[(here + step) % cycle] > 0
        best = jnp.maximum(best, jnp.where(live, home[step] * scale[:, 0], jnp.float32(-2.0)))
    return best, sums, counts


def solution(mesh):
    placed = (
        P(("blk", "slab"), None),
        P("blk", None),
        P(),
        P(("blk", "slab")),
        P(("blk", "slab"), None),
        P(("blk", "slab")),
    )
    return jax.shard_map(
        per_device,
        mesh=mesh,
        in_specs=placed,
        out_specs=(P(("blk", "slab")), P(("blk", "slab"), None), P(("blk", "slab"))),
        check_vma=False,
    )
```

```python
import jax
import jax.numpy as jnp
from jax import lax
from jax.sharding import PartitionSpec as P


CL_DEV = 16
EPS = 1e-06
PIECES = 2
LANES = 128


def shifted(value, axis, steps):
    count = lax.axis_size(axis)
    pairs = [(source, (source + steps) % count) for source in range(count)]
    return lax.ppermute(value, axis, pairs)


def swapped(value, axis, bit):
    count = lax.axis_size(axis)
    return lax.ppermute(value, axis, [(source, source ^ bit) for source in range(count)])


def inverse_norm(values):
    wide = values.astype(jnp.float32)
    return lax.rsqrt(jnp.sum(wide * wide, axis=-1, keepdims=True) + EPS)


def halvings(lanes):
    return lanes.bit_length() - 1


def kept_sums(new_unit, kept_row, owner, kept_local):
    cycle = lax.axis_size("blk")
    lanes = lax.axis_size("slab")
    here = lax.axis_index("blk")
    lane = lax.axis_index("slab")
    rows, width = new_unit.shape
    entries = kept_row.shape[0]
    levels = halvings(lanes)
    pick = (kept_row[:, None] == jnp.arange(rows, dtype=jnp.int32)[None, :]).astype(jnp.bfloat16)
    picked = jnp.dot(pick, new_unit, preferred_element_type=jnp.float32).astype(jnp.bfloat16)
    picked = jnp.concatenate([picked, jnp.ones((entries, LANES), jnp.bfloat16)], axis=1)
    apart = (owner % lanes) ^ lane
    mirrored = jnp.zeros_like(apart)
    for level in range(levels):
        mirrored = mirrored * 2 + ((apart >> level) & 1)
    ahead = (owner // lanes - here) % cycle
    place = (mirrored * cycle + ahead) * CL_DEV + kept_local
    total = lanes * cycle * CL_DEV
    spread = (jnp.arange(total, dtype=jnp.int32)[:, None] == place[None, :]).astype(jnp.bfloat16)
    half = total // 2
    keep = jnp.dot(spread[:half], picked, preferred_element_type=jnp.float32)
    send = jnp.dot(spread[half:], picked, preferred_element_type=jnp.float32)
    for level in range(levels):
        got = swapped(send, "slab", 1 << level)
        whole = keep + got
        half = whole.shape[0] // 2
        keep, send = whole[:half], whole[half:]
    parts = [whole[:CL_DEV]]
    for step in range(1, cycle):
        part = whole[step * CL_DEV : (step + 1) * CL_DEV].astype(jnp.bfloat16)
        parts.append(shifted(part, "blk", step))
    sums = parts[0]
    for part in parts[1:]:
        sums = sums + part.astype(jnp.float32)
    return sums[:, :width], sums[:, width]


def per_device(new_rows, index_rows, pattern, kept_row, kept_owner, kept_local):
    cycle = lax.axis_size("blk")
    lanes = lax.axis_size("slab")
    here = lax.axis_index("blk")
    lane = lax.axis_index("slab")
    rows = new_rows.shape[0]
    index_scale = inverse_norm(index_rows)[:, 0]

    def tile_max(block):
        scores = lax.dot_general(
            block, index_rows, (((1,), (1,)), ((), ())), preferred_element_type=jnp.float32
        )
        return jnp.max(scores * index_scale[None, :], axis=1)

    piece = rows // PIECES
    moving = [new_rows[:piece]]
    kept_apart = lax.optimization_barrier(new_rows)
    moving += [kept_apart[i * piece : (i + 1) * piece] for i in range(1, PIECES)]
    home = [tile_max(new_rows)]
    for step in range(1, cycle):
        tops = []
        for i in range(PIECES):
            moving[i] = shifted(moving[i], "blk", 1)
            tops.append(tile_max(moving[i]))
        home.append(shifted(jnp.concatenate(tops), "blk", -step))
    scale = lax.optimization_barrier(inverse_norm(new_rows))
    sums, counts = kept_sums(
        (new_rows.astype(jnp.float32) * scale).astype(jnp.bfloat16),
        kept_row,
        kept_owner[:, 0],
        kept_local,
    )
    wanted = (here + jnp.arange(cycle, dtype=jnp.int32)) % cycle
    mine = (jnp.arange(cycle * lanes, dtype=jnp.int32) == here * lanes + lane)[None, :, None] & (
        jnp.arange(cycle, dtype=jnp.int32)[None, None, :] == wanted[:, None, None]
    )
    live = jnp.max(jnp.where(mine, pattern[None], 0), axis=(1, 2))
    live = lax.optimization_barrier(jnp.broadcast_to(live[:, None], (cycle, rows)))

    def masked(step):
        return jnp.where(live[step] > 0, home[step] * scale[:, 0], jnp.float32(-2.0))

    best = masked(0)
    for step in range(1, cycle - 1):
        best = jnp.maximum(best, masked(step))
    best = lax.optimization_barrier(best)
    best = jnp.maximum(best, masked(cycle - 1))
    return best, sums, counts


def solution(mesh):
    placed = (
        P(("blk", "slab"), None),
        P("blk", None),
        P(),
        P(("blk", "slab")),
        P(("blk", "slab"), None),
        P(("blk", "slab")),
    )
    return jax.shard_map(
        per_device,
        mesh=mesh,
        in_specs=placed,
        out_specs=(P(("blk", "slab")), P(("blk", "slab"), None), P(("blk", "slab"))),
        check_vma=False,
    )
```

```python
import jax
import jax.numpy as jnp
from jax import lax
from jax.experimental import pallas as pl
from jax.experimental.pallas import tpu as pltpu
from jax.sharding import PartitionSpec as P


CL_DEV = 16
EPS = 1e-06
SPLIT = (1, 1)
PIECES = len(SPLIT)
PREPARE_VMEM = 24 << 20
LANES = 128


def order_of(count):
    return list(range(0, count, 2)) + list(range(count - 1 - count % 2, 0, -2))


def plane_at(place, count):
    return jnp.where(2 * place < count, 2 * place, 2 * (count - 1 - place) + 1)


def place_of(plane, count):
    return jnp.where(plane & 1 == 0, plane >> 1, count - 1 - (plane >> 1))


def shifted(value, axis, steps):
    count = lax.axis_size(axis)
    ring = order_of(count)
    pairs = [(ring[i], ring[(i + steps) % count]) for i in range(count)]
    return lax.ppermute(value, axis, pairs)


def swapped(value, axis, bit):
    count = lax.axis_size(axis)
    return lax.ppermute(value, axis, [(source, source ^ bit) for source in range(count)])


def inverse_norm(values):
    wide = values.astype(jnp.float32)
    return lax.rsqrt(jnp.sum(wide * wide, axis=-1, keepdims=True) + EPS)


def halvings(lanes):
    return lanes.bit_length() - 1


def prepare_body(cycle, lanes, rows_ref, row_ref, owner_ref, local_ref, pattern_ref, *outs):
    keep_ref, send_ref, scale_ref, live_ref = outs
    here = lax.axis_index("blk")
    lane = lax.axis_index("slab")
    rows, width = rows_ref.shape
    entries = row_ref.shape[1]
    levels = halvings(lanes)
    mask = cycle - 1
    spot = place_of(here, cycle)
    wide = rows_ref[...].astype(jnp.float32)
    scale = lax.rsqrt(jnp.sum(wide * wide, axis=-1, keepdims=True) + EPS)
    unit = (wide * scale).astype(jnp.bfloat16)
    scale_ref[...] = jnp.transpose(jnp.broadcast_to(scale, (rows, LANES)))[:1]
    owner = owner_ref[...]
    apart = (owner & (lanes - 1)) ^ lane
    mirrored = jnp.zeros_like(apart)
    for level in range(levels):
        mirrored = mirrored * 2 + ((apart >> level) & 1)
    ahead = (place_of(owner >> levels, cycle) - spot + cycle) & mask
    place = (mirrored * cycle + ahead) * CL_DEV + local_ref[...]
    total = lanes * cycle * CL_DEV
    spread = (lax.broadcasted_iota(jnp.int32, (total, entries), 0) == place).astype(jnp.bfloat16)
    picks = lax.broadcasted_iota(jnp.int32, (rows, entries), 0) == row_ref[...]
    weight = lax.dot_general(
        spread,
        picks.astype(jnp.bfloat16),
        (((1,), (1,)), ((), ())),
        preferred_element_type=jnp.float32,
    ).astype(jnp.bfloat16)
    sums = jnp.dot(weight, unit, preferred_element_type=jnp.float32)
    ones = jnp.ones((entries, LANES), jnp.bfloat16)
    counts = jnp.dot(spread, ones, preferred_element_type=jnp.float32)
    half = total // 2
    keep_ref[:, :width] = sums[:half]
    keep_ref[:, width:] = counts[:half]
    send_ref[:, :width] = sums[half:]
    send_ref[:, width:] = counts[half:]
    pattern = pattern_ref[...]
    column = lax.broadcasted_iota(jnp.int32, pattern.shape, 1) == here * lanes + lane
    mine = jnp.sum(jnp.where(column, pattern, 0), axis=1, keepdims=True)
    span = lax.broadcasted_iota(jnp.int32, mine.shape, 0)
    for step in range(cycle):
        target = plane_at((spot + step) & mask, cycle)
        mark = jnp.sum(jnp.where(span == target, mine, 0), axis=0, keepdims=True)
        live_ref[step : step + 1, :] = jnp.broadcast_to(mark, (1, rows))


def prepare(new_rows, pattern, kept_row, kept_owner, kept_local):
    cycle = lax.axis_size("blk")
    lanes = lax.axis_size("slab")
    assert cycle & (cycle - 1) == 0 and lanes & (lanes - 1) == 0
    rows, width = new_rows.shape
    entries = kept_row.shape[0]
    half = lanes * cycle * CL_DEV // 2
    part = jax.ShapeDtypeStruct((half, width + LANES), jnp.float32)
    return pl.pallas_call(
        lambda *refs: prepare_body(cycle, lanes, *refs),
        out_shape=[
            part,
            part,
            jax.ShapeDtypeStruct((1, rows), jnp.float32),
            jax.ShapeDtypeStruct((cycle, rows), jnp.int32),
        ],
        compiler_params=pltpu.CompilerParams(vmem_limit_bytes=PREPARE_VMEM),
        cost_estimate=pl.CostEstimate(
            flops=4 * half * (entries * rows + rows * width + entries * LANES),
            bytes_accessed=2 * rows * width + 8 * half * (width + LANES),
            transcendentals=rows,
        ),
        name="prepare",
    )(
        new_rows,
        kept_row[None, :],
        kept_owner[:, 0][None, :],
        kept_local[None, :],
        pattern.T,
    )


def kept_sums(keep, send):
    cycle = lax.axis_size("blk")
    lanes = lax.axis_size("slab")
    width = keep.shape[1] - LANES
    for level in range(halvings(lanes)):
        got = swapped(send, "slab", 1 << level)
        whole = keep + got
        half = whole.shape[0] // 2
        keep, send = whole[:half], whole[half:]
    parts = [whole[:CL_DEV]]
    for step in range(1, cycle):
        part = whole[step * CL_DEV : (step + 1) * CL_DEV].astype(jnp.bfloat16)
        parts.append(shifted(part, "blk", step))
    sums = parts[0]
    for part in parts[1:]:
        sums = sums + part.astype(jnp.float32)
    return sums[:, :width], sums[:, width]


def per_device(new_rows, index_rows, pattern, kept_row, kept_owner, kept_local):
    cycle = lax.axis_size("blk")
    rows = new_rows.shape[0]
    index_scale = inverse_norm(index_rows)[:, 0]

    def tile_max(block):
        scores = lax.dot_general(
            block, index_rows, (((1,), (1,)), ((), ())), preferred_element_type=jnp.float32
        )
        return jnp.max(scores * index_scale[None, :], axis=1)

    ends = [rows * sum(SPLIT[: i + 1]) // sum(SPLIT) for i in range(PIECES)]
    moving = [new_rows[: ends[0]]]
    kept_apart = lax.optimization_barrier(new_rows)
    moving += [kept_apart[low:high] for low, high in zip(ends, ends[1:])]
    home = [tile_max(new_rows)]
    for step in range(1, cycle):
        tops = []
        for i in range(PIECES):
            moving[i] = shifted(moving[i], "blk", 1)
            tops.append(tile_max(moving[i]))
        home.append(shifted(jnp.concatenate(tops), "blk", -step))
    keep, send, scale, live = prepare(new_rows, pattern, kept_row, kept_owner, kept_local)
    sums, counts = kept_sums(keep, send)

    def masked(step):
        return jnp.where(live[step] > 0, home[step] * scale[0], jnp.float32(-2.0))

    best = masked(0)
    for step in range(1, cycle - 1):
        best = jnp.maximum(best, masked(step))
    best = lax.optimization_barrier(best)
    best = jnp.maximum(best, masked(cycle - 1))
    return best, sums, counts


def solution(mesh):
    placed = (
        P(("blk", "slab"), None),
        P("blk", None),
        P(),
        P(("blk", "slab")),
        P(("blk", "slab"), None),
        P(("blk", "slab")),
    )
    return jax.shard_map(
        per_device,
        mesh=mesh,
        in_specs=placed,
        out_specs=(P(("blk", "slab")), P(("blk", "slab"), None), P(("blk", "slab"))),
        check_vma=False,
    )
```

```python
import jax
import jax.numpy as jnp
from jax import lax
from jax.experimental import pallas as pl
from jax.experimental.pallas import tpu as pltpu
from jax.sharding import PartitionSpec as P


CL_DEV = 16
EPS = 1e-06
SPLIT = (1, 1)
PIECES = len(SPLIT)
PREPARE_VMEM = 24 << 20
LANES = 128


def order_of(count):
    return list(range(0, count, 2)) + list(range(count - 1 - count % 2, 0, -2))


def plane_at(place, count):
    return jnp.where(2 * place < count, 2 * place, 2 * (count - 1 - place) + 1)


def place_of(plane, count):
    return jnp.where(plane & 1 == 0, plane >> 1, count - 1 - (plane >> 1))


def shifted(value, axis, steps):
    count = lax.axis_size(axis)
    ring = order_of(count)
    pairs = [(ring[i], ring[(i + steps) % count]) for i in range(count)]
    return lax.ppermute(value, axis, pairs)


def swapped(value, axis, bit):
    count = lax.axis_size(axis)
    return lax.ppermute(value, axis, [(source, source ^ bit) for source in range(count)])


def inverse_norm(values):
    wide = values.astype(jnp.float32)
    return lax.rsqrt(jnp.sum(wide * wide, axis=-1, keepdims=True) + EPS)


def halvings(lanes):
    return lanes.bit_length() - 1


def prepare_body(cycle, lanes, rows_ref, row_ref, owner_ref, local_ref, pattern_ref, *outs):
    keep_ref, send_ref, scale_ref, live_ref = outs
    here = lax.axis_index("blk")
    lane = lax.axis_index("slab")
    rows, width = rows_ref.shape
    entries = row_ref.shape[1]
    levels = halvings(lanes)
    mask = cycle - 1
    spot = place_of(here, cycle)
    wide = rows_ref[...].astype(jnp.float32)
    scale = lax.rsqrt(jnp.sum(wide * wide, axis=-1, keepdims=True) + EPS)
    unit = (wide * scale).astype(jnp.bfloat16)
    scale_ref[...] = jnp.transpose(jnp.broadcast_to(scale, (rows, LANES)))[:1]
    owner = owner_ref[...]
    apart = (owner & (lanes - 1)) ^ lane
    mirrored = jnp.zeros_like(apart)
    for level in range(levels):
        mirrored = mirrored * 2 + ((apart >> level) & 1)
    ahead = (place_of(owner >> levels, cycle) - spot + cycle) & mask
    place = (mirrored * cycle + ahead) * CL_DEV + local_ref[...]
    total = lanes * cycle * CL_DEV
    spread = (lax.broadcasted_iota(jnp.int32, (total, entries), 0) == place).astype(jnp.bfloat16)
    picks = lax.broadcasted_iota(jnp.int32, (rows, entries), 0) == row_ref[...]
    weight = lax.dot_general(
        spread,
        picks.astype(jnp.bfloat16),
        (((1,), (1,)), ((), ())),
        preferred_element_type=jnp.float32,
    ).astype(jnp.bfloat16)
    sums = jnp.dot(weight, unit, preferred_element_type=jnp.float32)
    ones = jnp.ones((entries, LANES), jnp.bfloat16)
    counts = jnp.dot(spread, ones, preferred_element_type=jnp.float32)
    half = total // 2
    keep_ref[:, :width] = sums[:half]
    keep_ref[:, width:] = counts[:half]
    send_ref[:, :width] = sums[half:]
    send_ref[:, width:] = counts[half:]
    pattern = pattern_ref[...]
    column = lax.broadcasted_iota(jnp.int32, pattern.shape, 1) == here * lanes + lane
    mine = jnp.sum(jnp.where(column, pattern, 0), axis=1, keepdims=True)
    span = lax.broadcasted_iota(jnp.int32, mine.shape, 0)
    for step in range(cycle):
        target = plane_at((spot + step) & mask, cycle)
        mark = jnp.sum(jnp.where(span == target, mine, 0), axis=0, keepdims=True)
        live_ref[step : step + 1, :] = jnp.broadcast_to(mark, (1, rows))


def prepare(new_rows, pattern, kept_row, kept_owner, kept_local):
    cycle = lax.axis_size("blk")
    lanes = lax.axis_size("slab")
    assert cycle & (cycle - 1) == 0 and lanes & (lanes - 1) == 0
    rows, width = new_rows.shape
    entries = kept_row.shape[0]
    half = lanes * cycle * CL_DEV // 2
    part = jax.ShapeDtypeStruct((half, width + LANES), jnp.float32)
    return pl.pallas_call(
        lambda *refs: prepare_body(cycle, lanes, *refs),
        out_shape=[
            part,
            part,
            jax.ShapeDtypeStruct((1, rows), jnp.float32),
            jax.ShapeDtypeStruct((cycle, rows), jnp.int32),
        ],
        compiler_params=pltpu.CompilerParams(vmem_limit_bytes=PREPARE_VMEM),
        cost_estimate=pl.CostEstimate(
            flops=4 * half * (entries * rows + rows * width + entries * LANES),
            bytes_accessed=2 * rows * width + 8 * half * (width + LANES),
            transcendentals=rows,
        ),
        name="prepare",
    )(
        new_rows,
        kept_row[None, :],
        kept_owner[:, 0][None, :],
        kept_local[None, :],
        pattern.T,
    )


def kept_sums(keep, send):
    cycle = lax.axis_size("blk")
    lanes = lax.axis_size("slab")
    for level in range(halvings(lanes)):
        got = swapped(send, "slab", 1 << level)
        whole = keep + got
        half = whole.shape[0] // 2
        keep, send = whole[:half], whole[half:]
    parts = [whole[:CL_DEV]]
    for step in range(1, cycle):
        part = whole[step * CL_DEV : (step + 1) * CL_DEV]
        parts.append(shifted(part, "blk", step))
    return parts


def finish_body(cycle, *refs):
    parts, tops = refs[:cycle], refs[cycle : 2 * cycle - 1]
    scale_ref, live_ref, sums_ref, counts_ref, early_ref = refs[2 * cycle - 1 :]
    width = sums_ref.shape[1]
    total = parts[0][...]
    for part in parts[1:]:
        total = total + part[...].astype(jnp.float32)
    sums_ref[...] = total[:, :width]
    counts_ref[...] = jnp.transpose(total[:, width:])[:1]
    best = jnp.full(early_ref.shape, -2.0, jnp.float32)
    for step, top in enumerate(tops):
        value = jnp.where(live_ref[step : step + 1, :] > 0, top[...] * scale_ref[...], -2.0)
        best = jnp.maximum(best, value)
    early_ref[...] = best


def finish(parts, tops, scale, live):
    cycle = len(parts)
    width = parts[0].shape[1] - LANES
    return pl.pallas_call(
        lambda *refs: finish_body(cycle, *refs),
        out_shape=[
            jax.ShapeDtypeStruct((CL_DEV, width), jnp.float32),
            jax.ShapeDtypeStruct((1, CL_DEV), jnp.float32),
            jax.ShapeDtypeStruct(scale.shape, jnp.float32),
        ],
        compiler_params=pltpu.CompilerParams(vmem_limit_bytes=8 << 20),
        cost_estimate=pl.CostEstimate(
            flops=2 * cycle * CL_DEV * width,
            bytes_accessed=4 * cycle * CL_DEV * width,
            transcendentals=0,
        ),
        name="finish",
    )(*parts, *[top[None, :] for top in tops], scale, live)


def per_device(new_rows, index_rows, pattern, kept_row, kept_owner, kept_local):
    cycle = lax.axis_size("blk")
    rows = new_rows.shape[0]
    index_scale = inverse_norm(index_rows)[:, 0]

    def tile_max(block):
        scores = lax.dot_general(
            block, index_rows, (((1,), (1,)), ((), ())), preferred_element_type=jnp.float32
        )
        return jnp.max(scores * index_scale[None, :], axis=1)

    ends = [rows * sum(SPLIT[: i + 1]) // sum(SPLIT) for i in range(PIECES)]
    moving = [new_rows[: ends[0]]]
    kept_apart = lax.optimization_barrier(new_rows)
    moving += [kept_apart[low:high] for low, high in zip(ends, ends[1:])]
    home = [tile_max(new_rows)]
    for step in range(1, cycle):
        tops = []
        for i in range(PIECES):
            moving[i] = shifted(moving[i], "blk", 1)
            tops.append(tile_max(moving[i]))
        home.append(shifted(jnp.concatenate(tops), "blk", -step))
    keep, send, scale, live = prepare(new_rows, pattern, kept_row, kept_owner, kept_local)
    parts = kept_sums(keep, send)
    sums, counts, early = finish(parts, home[:-1], scale, live)
    last = jnp.where(live[cycle - 1] > 0, home[-1] * scale[0], jnp.float32(-2.0))
    return jnp.maximum(early[0], last), sums, counts[0]


def solution(mesh):
    placed = (
        P(("blk", "slab"), None),
        P("blk", None),
        P(),
        P(("blk", "slab")),
        P(("blk", "slab"), None),
        P(("blk", "slab")),
    )
    return jax.shard_map(
        per_device,
        mesh=mesh,
        in_specs=placed,
        out_specs=(P(("blk", "slab")), P(("blk", "slab"), None), P(("blk", "slab"))),
        check_vma=False,
    )
```

```python
import jax
import jax.numpy as jnp
from jax import lax
from jax.experimental import pallas as pl
from jax.experimental.pallas import tpu as pltpu
from jax.sharding import PartitionSpec as P


CL_DEV = 16
EPS = 1e-06
PIECES = 2
PREPARE_VMEM = 24 << 20
LANES = 128


def order_of(count):
    return list(range(0, count, 2)) + list(range(count - 1 - count % 2, 0, -2))


def plane_at(place, count):
    return jnp.where(2 * place < count, 2 * place, 2 * (count - 1 - place) + 1)


def place_of(plane, count):
    return jnp.where(plane & 1 == 0, plane >> 1, count - 1 - (plane >> 1))


def shifted(value, axis, steps):
    count = lax.axis_size(axis)
    ring = order_of(count)
    pairs = [(ring[i], ring[(i + steps) % count]) for i in range(count)]
    return lax.ppermute(value, axis, pairs)


def swapped(value, axis, bit):
    count = lax.axis_size(axis)
    return lax.ppermute(value, axis, [(source, source ^ bit) for source in range(count)])


def inverse_norm(values):
    wide = values.astype(jnp.float32)
    return lax.rsqrt(jnp.sum(wide * wide, axis=-1, keepdims=True) + EPS)


def halvings(lanes):
    return lanes.bit_length() - 1


def prepare_body(cycle, lanes, rows_ref, row_ref, owner_ref, local_ref, pattern_ref, *outs):
    keep_ref, send_ref, scale_ref, live_ref = outs
    here = lax.axis_index("blk")
    lane = lax.axis_index("slab")
    rows, width = rows_ref.shape
    entries = row_ref.shape[1]
    levels = halvings(lanes)
    mask = cycle - 1
    spot = place_of(here, cycle)
    wide = rows_ref[...].astype(jnp.float32)
    scale = lax.rsqrt(jnp.sum(wide * wide, axis=-1, keepdims=True) + EPS)
    unit = (wide * scale).astype(jnp.bfloat16)
    scale_ref[...] = jnp.transpose(jnp.broadcast_to(scale, (rows, LANES)))[:1]
    owner = owner_ref[...]
    apart = (owner & (lanes - 1)) ^ lane
    mirrored = jnp.zeros_like(apart)
    for level in range(levels):
        mirrored = mirrored * 2 + ((apart >> level) & 1)
    ahead = (place_of(owner >> levels, cycle) - spot + cycle) & mask
    place = (mirrored * cycle + ahead) * CL_DEV + local_ref[...]
    total = lanes * cycle * CL_DEV
    spread = (lax.broadcasted_iota(jnp.int32, (total, entries), 0) == place).astype(jnp.bfloat16)
    picks = lax.broadcasted_iota(jnp.int32, (rows, entries), 0) == row_ref[...]
    weight = lax.dot_general(
        spread,
        picks.astype(jnp.bfloat16),
        (((1,), (1,)), ((), ())),
        preferred_element_type=jnp.float32,
    ).astype(jnp.bfloat16)
    sums = jnp.dot(weight, unit, preferred_element_type=jnp.float32)
    ones = jnp.ones((entries, LANES), jnp.bfloat16)
    counts = jnp.dot(spread, ones, preferred_element_type=jnp.float32)
    half = total // 2
    keep_ref[:, :width] = sums[:half]
    keep_ref[:, width:] = counts[:half]
    send_ref[:, :width] = sums[half:]
    send_ref[:, width:] = counts[half:]
    pattern = pattern_ref[...]
    column = lax.broadcasted_iota(jnp.int32, pattern.shape, 1) == here * lanes + lane
    mine = jnp.sum(jnp.where(column, pattern, 0), axis=1, keepdims=True)
    span = lax.broadcasted_iota(jnp.int32, mine.shape, 0)
    for step in range(cycle):
        target = plane_at((spot + step) & mask, cycle)
        mark = jnp.sum(jnp.where(span == target, mine, 0), axis=0, keepdims=True)
        live_ref[step : step + 1, :] = jnp.broadcast_to(mark, (1, rows))


def prepare(new_rows, pattern, kept_row, kept_owner, kept_local):
    cycle = lax.axis_size("blk")
    lanes = lax.axis_size("slab")
    assert cycle & (cycle - 1) == 0 and lanes & (lanes - 1) == 0
    rows, width = new_rows.shape
    entries = kept_row.shape[0]
    half = lanes * cycle * CL_DEV // 2
    part = jax.ShapeDtypeStruct((half, width + LANES), jnp.float32)
    return pl.pallas_call(
        lambda *refs: prepare_body(cycle, lanes, *refs),
        out_shape=[
            part,
            part,
            jax.ShapeDtypeStruct((1, rows), jnp.float32),
            jax.ShapeDtypeStruct((cycle, rows), jnp.int32),
        ],
        compiler_params=pltpu.CompilerParams(vmem_limit_bytes=PREPARE_VMEM),
        cost_estimate=pl.CostEstimate(
            flops=4 * half * (entries * rows + rows * width + entries * LANES),
            bytes_accessed=2 * rows * width + 8 * half * (width + LANES),
            transcendentals=rows,
        ),
        name="prepare",
    )(
        new_rows,
        kept_row[None, :],
        kept_owner[:, 0][None, :],
        kept_local[None, :],
        pattern.T,
    )


def kept_sums(keep, send):
    cycle = lax.axis_size("blk")
    lanes = lax.axis_size("slab")
    for level in range(halvings(lanes)):
        got = swapped(send, "slab", 1 << level)
        whole = keep + got
        half = whole.shape[0] // 2
        keep, send = whole[:half], whole[half:]
    parts = [whole[:CL_DEV]]
    for step in range(1, cycle):
        part = whole[step * CL_DEV : (step + 1) * CL_DEV].astype(jnp.bfloat16)
        parts.append(shifted(part, "blk", step))
    return parts


def finish_body(cycle, *refs):
    parts, tops = refs[:cycle], refs[cycle : 2 * cycle - 1]
    scale_ref, live_ref, sums_ref, counts_ref, early_ref = refs[2 * cycle - 1 :]
    width = sums_ref.shape[1]
    total = parts[0][...]
    for part in parts[1:]:
        total = total + part[...].astype(jnp.float32)
    sums_ref[...] = total[:, :width]
    counts_ref[...] = jnp.transpose(total[:, width:])[:1]
    best = jnp.full(early_ref.shape, -2.0, jnp.float32)
    for step, top in enumerate(tops):
        value = jnp.where(live_ref[step : step + 1, :] > 0, top[...] * scale_ref[...], -2.0)
        best = jnp.maximum(best, value)
    early_ref[...] = best


def finish(parts, tops, scale, live):
    cycle = len(parts)
    width = parts[0].shape[1] - LANES
    return pl.pallas_call(
        lambda *refs: finish_body(cycle, *refs),
        out_shape=[
            jax.ShapeDtypeStruct((CL_DEV, width), jnp.float32),
            jax.ShapeDtypeStruct((1, CL_DEV), jnp.float32),
            jax.ShapeDtypeStruct(scale.shape, jnp.float32),
        ],
        compiler_params=pltpu.CompilerParams(vmem_limit_bytes=8 << 20),
        cost_estimate=pl.CostEstimate(
            flops=2 * cycle * CL_DEV * width,
            bytes_accessed=4 * cycle * CL_DEV * width,
            transcendentals=0,
        ),
        name="finish",
    )(*parts, *[top[None, :] for top in tops], scale, live)


def per_device(new_rows, index_rows, pattern, kept_row, kept_owner, kept_local):
    cycle = lax.axis_size("blk")
    rows = new_rows.shape[0]
    index_scale = inverse_norm(index_rows)[:, 0]

    def tile_max(block):
        scores = lax.dot_general(
            block, index_rows, (((1,), (1,)), ((), ())), preferred_element_type=jnp.float32
        )
        return jnp.max(scores * index_scale[None, :], axis=1)

    half = rows // PIECES
    home = [tile_max(new_rows)]
    arrived = shifted(new_rows, "blk", 1)
    top = tile_max(arrived)
    home.append(shifted(top, "blk", -1))
    second = shifted(lax.optimization_barrier(new_rows)[half:], "blk", -1)
    second_top = tile_max(second)
    moving = [arrived[:half], arrived[half:]]
    for step in range(2, cycle):
        if step == cycle - 1:
            moving.pop()
        tops = []
        for i in range(len(moving)):
            moving[i] = shifted(moving[i], "blk", 1)
            tops.append(tile_max(moving[i]))
        if step == cycle - 1:
            tops.append(second_top)
        home.append(shifted(jnp.concatenate(tops), "blk", -step))
    keep, send, scale, live = prepare(new_rows, pattern, kept_row, kept_owner, kept_local)
    parts = kept_sums(keep, send)
    sums, counts, early = finish(parts, home[:-1], scale, live)
    last = jnp.where(live[cycle - 1] > 0, home[-1] * scale[0], jnp.float32(-2.0))
    return jnp.maximum(early[0], last), sums, counts[0]


def solution(mesh):
    placed = (
        P(("blk", "slab"), None),
        P("blk", None),
        P(),
        P(("blk", "slab")),
        P(("blk", "slab"), None),
        P(("blk", "slab")),
    )
    return jax.shard_map(
        per_device,
        mesh=mesh,
        in_specs=placed,
        out_specs=(P(("blk", "slab")), P(("blk", "slab"), None), P(("blk", "slab"))),
        check_vma=False,
    )
```

```python
import jax
import jax.numpy as jnp
from jax import lax
from jax.experimental import pallas as pl
from jax.experimental.pallas import tpu as pltpu
from jax.sharding import PartitionSpec as P


CL_DEV = 16
EPS = 1e-06
PIECES = 2
PREPARE_VMEM = 24 << 20
LANES = 128


def order_of(count):
    return list(range(0, count, 2)) + list(range(count - 1 - count % 2, 0, -2))


def plane_at(place, count):
    return jnp.where(2 * place < count, 2 * place, 2 * (count - 1 - place) + 1)


def place_of(plane, count):
    return jnp.where(plane & 1 == 0, plane >> 1, count - 1 - (plane >> 1))


def shifted(value, axis, steps):
    count = lax.axis_size(axis)
    ring = order_of(count)
    pairs = [(ring[i], ring[(i + steps) % count]) for i in range(count)]
    return lax.ppermute(value, axis, pairs)


def swapped(value, axis, bit):
    count = lax.axis_size(axis)
    return lax.ppermute(value, axis, [(source, source ^ bit) for source in range(count)])


def inverse_norm(values):
    wide = values.astype(jnp.float32)
    return lax.rsqrt(jnp.sum(wide * wide, axis=-1, keepdims=True) + EPS)


def halvings(lanes):
    return lanes.bit_length() - 1


def prepare_body(cycle, lanes, rows_ref, row_ref, owner_ref, local_ref, pattern_ref, *outs):
    keep_ref, send_ref, scale_ref, live_ref = outs
    here = lax.axis_index("blk")
    lane = lax.axis_index("slab")
    rows, width = rows_ref.shape
    entries = row_ref.shape[1]
    levels = halvings(lanes)
    mask = cycle - 1
    spot = place_of(here, cycle)
    wide = rows_ref[...].astype(jnp.float32)
    scale = lax.rsqrt(jnp.sum(wide * wide, axis=-1, keepdims=True) + EPS)
    unit = (wide * scale).astype(jnp.bfloat16)
    scale_ref[...] = jnp.transpose(jnp.broadcast_to(scale, (rows, LANES)))[:1]
    owner = owner_ref[...]
    apart = (owner & (lanes - 1)) ^ lane
    mirrored = jnp.zeros_like(apart)
    for level in range(levels):
        mirrored = mirrored * 2 + ((apart >> level) & 1)
    ahead = (place_of(owner >> levels, cycle) - spot + cycle) & mask
    place = (mirrored * cycle + ahead) * CL_DEV + local_ref[...]
    total = lanes * cycle * CL_DEV
    spread = (lax.broadcasted_iota(jnp.int32, (total, entries), 0) == place).astype(jnp.bfloat16)
    picks = lax.broadcasted_iota(jnp.int32, (rows, entries), 0) == row_ref[...]
    weight = lax.dot_general(
        spread,
        picks.astype(jnp.bfloat16),
        (((1,), (1,)), ((), ())),
        preferred_element_type=jnp.float32,
    ).astype(jnp.bfloat16)
    sums = jnp.dot(weight, unit, preferred_element_type=jnp.float32)
    ones = jnp.ones((entries, LANES), jnp.bfloat16)
    counts = jnp.dot(spread, ones, preferred_element_type=jnp.float32)
    half = total // 2
    keep_ref[:, :width] = sums[:half]
    keep_ref[:, width:] = counts[:half]
    send_ref[:, :width] = sums[half:]
    send_ref[:, width:] = counts[half:]
    pattern = pattern_ref[...]
    column = lax.broadcasted_iota(jnp.int32, pattern.shape, 1) == here * lanes + lane
    mine = jnp.sum(jnp.where(column, pattern, 0), axis=1, keepdims=True)
    span = lax.broadcasted_iota(jnp.int32, mine.shape, 0)
    for step in range(cycle):
        target = plane_at((spot + step) & mask, cycle)
        mark = jnp.sum(jnp.where(span == target, mine, 0), axis=0, keepdims=True)
        live_ref[step : step + 1, :] = jnp.broadcast_to(mark, (1, rows))


def prepare(new_rows, pattern, kept_row, kept_owner, kept_local):
    cycle = lax.axis_size("blk")
    lanes = lax.axis_size("slab")
    assert cycle & (cycle - 1) == 0 and lanes & (lanes - 1) == 0
    rows, width = new_rows.shape
    entries = kept_row.shape[0]
    half = lanes * cycle * CL_DEV // 2
    part = jax.ShapeDtypeStruct((half, width + LANES), jnp.float32)
    return pl.pallas_call(
        lambda *refs: prepare_body(cycle, lanes, *refs),
        out_shape=[
            part,
            part,
            jax.ShapeDtypeStruct((1, rows), jnp.float32),
            jax.ShapeDtypeStruct((cycle, rows), jnp.int32),
        ],
        compiler_params=pltpu.CompilerParams(vmem_limit_bytes=PREPARE_VMEM),
        cost_estimate=pl.CostEstimate(
            flops=4 * half * (entries * rows + rows * width + entries * LANES),
            bytes_accessed=2 * rows * width + 8 * half * (width + LANES),
            transcendentals=rows,
        ),
        name="prepare",
    )(
        pltpu.with_memory_space_constraint(new_rows, pltpu.HBM),
        *[
            pltpu.with_memory_space_constraint(value, pltpu.HBM)
            for value in (kept_row[None, :], kept_owner[:, 0][None, :], kept_local[None, :])
        ],
        pltpu.with_memory_space_constraint(pattern.T, pltpu.HBM),
    )


def kept_sums(keep, send):
    cycle = lax.axis_size("blk")
    lanes = lax.axis_size("slab")
    for level in range(halvings(lanes)):
        got = swapped(send, "slab", 1 << level)
        whole = keep + got
        half = whole.shape[0] // 2
        keep, send = whole[:half], whole[half:]
    parts = [whole[:CL_DEV]]
    for step in range(1, cycle):
        part = whole[step * CL_DEV : (step + 1) * CL_DEV].astype(jnp.bfloat16)
        parts.append(shifted(part, "blk", step))
    return parts


def finish_body(cycle, *refs):
    parts, tops = refs[:cycle], refs[cycle : 2 * cycle - 1]
    scale_ref, live_ref, sums_ref, counts_ref, early_ref = refs[2 * cycle - 1 :]
    width = sums_ref.shape[1]
    total = parts[0][...]
    for part in parts[1:]:
        total = total + part[...].astype(jnp.float32)
    sums_ref[...] = total[:, :width]
    counts_ref[...] = jnp.transpose(total[:, width:])[:1]
    best = jnp.full(early_ref.shape, -2.0, jnp.float32)
    for step, top in enumerate(tops):
        value = jnp.where(live_ref[step : step + 1, :] > 0, top[...] * scale_ref[...], -2.0)
        best = jnp.maximum(best, value)
    early_ref[...] = best


def finish(parts, tops, scale, live):
    cycle = len(parts)
    width = parts[0].shape[1] - LANES
    return pl.pallas_call(
        lambda *refs: finish_body(cycle, *refs),
        out_shape=[
            jax.ShapeDtypeStruct((CL_DEV, width), jnp.float32),
            jax.ShapeDtypeStruct((1, CL_DEV), jnp.float32),
            jax.ShapeDtypeStruct(scale.shape, jnp.float32),
        ],
        compiler_params=pltpu.CompilerParams(vmem_limit_bytes=8 << 20),
        cost_estimate=pl.CostEstimate(
            flops=2 * cycle * CL_DEV * width,
            bytes_accessed=4 * cycle * CL_DEV * width,
            transcendentals=0,
        ),
        name="finish",
    )(*parts, *[top[None, :] for top in tops], scale, live)


def per_device(new_rows, index_rows, pattern, kept_row, kept_owner, kept_local):
    cycle = lax.axis_size("blk")
    rows = new_rows.shape[0]
    index_scale = inverse_norm(index_rows)[:, 0]

    def tile_max(block):
        scores = lax.dot_general(
            block, index_rows, (((1,), (1,)), ((), ())), preferred_element_type=jnp.float32
        )
        return jnp.max(scores * index_scale[None, :], axis=1)

    half = rows // PIECES
    home = [tile_max(new_rows)]
    arrived = shifted(new_rows, "blk", 1)
    top = tile_max(arrived)
    home.append(shifted(top, "blk", -1))
    second = shifted(lax.optimization_barrier(new_rows)[half:], "blk", -1)
    second_top = tile_max(second)
    moving = [arrived[:half], arrived[half:]]
    for step in range(2, cycle):
        if step == cycle - 1:
            moving.pop()
        tops = []
        for i in range(len(moving)):
            moving[i] = shifted(moving[i], "blk", 1)
            tops.append(tile_max(moving[i]))
        if step == cycle - 1:
            tops.append(second_top)
        home.append(shifted(jnp.concatenate(tops), "blk", -step))
    keep, send, scale, live = prepare(new_rows, pattern, kept_row, kept_owner, kept_local)
    parts = kept_sums(keep, send)
    sums, counts, early = finish(parts, home[:-1], scale, live)
    last = jnp.where(live[cycle - 1] > 0, home[-1] * scale[0], jnp.float32(-2.0))
    return jnp.maximum(early[0], last), sums, counts[0]


def solution(mesh):
    placed = (
        P(("blk", "slab"), None),
        P("blk", None),
        P(),
        P(("blk", "slab")),
        P(("blk", "slab"), None),
        P(("blk", "slab")),
    )
    return jax.shard_map(
        per_device,
        mesh=mesh,
        in_specs=placed,
        out_specs=(P(("blk", "slab")), P(("blk", "slab"), None), P(("blk", "slab"))),
        check_vma=False,
    )
```
